32 devices in a mesh: mod: 4 (over z), frm: 2 (over x), ori: 4 (over y, core).
Axes of the slice: x: 2, y: 2, z: 4, core: 2. Of those that a mesh axis runs over, the one named last changes fastest.
Arguments:
- counts: int32 [512, 128, 128], P(('frm', 'ori'), 'mod'), may hold values from 0 to 8
- slice_codes: int32 [4096, 128, 128], P('ori', ('mod', 'frm')), may hold values from 0 to 2047
- pixel_mask: int32 [128, 128], P('mod'), may hold values 0 or 1
Outputs:
- log_posterior: float32 [2, 256, 4096], P('frm', 'mod', 'ori')
The draws below stay inside these ranges and needn't reach their ends.
All inputs are finite; a program needn't handle non-finite values. No bound on the sum of `pixel_mask` on one device may be relied on, other than what follows from the above.
Results may differ from the reference program's by a relative error of at most 0.0024.
Values may be sent and summed in bfloat16 or wider, within the bound.
A program may use at most 64 MiB of HBM per device.

```python
import math
import jax
import jax.numpy as jnp
from jax import lax

MCOLS = 128
ORIENT = 4096
PASSES = 8
FR_DEV = 64
ROWS = 128
FRAMES = 512
N_FRM = 2
N_ORI = 4


def draw_counts(key, part):
    level_key, pick_key, count_key = jax.random.split(key, 3)
    levels = jax.random.randint(level_key, (FRAMES,), 1, 9)
    brightest = jax.random.randint(pick_key, (), 0, FRAMES)
    levels = jnp.where(jnp.arange(FRAMES) == brightest, 8, levels)
    raw_values = jax.random.randint(count_key, (FRAMES, ROWS, MCOLS), 0, 65536)
    return (raw_values % (levels[:, None, None] + 1)).astype(jnp.int32)


def plant(array, stream_key, least, largest):
    index_at = [jax.random.randint(jax.random.fold_in(stream_key, axis), (), 0, length) for axis, length in enumerate(array.shape)]
    longest = array.shape.index(max(array.shape))
    next_to = index_at[:longest] + [(index_at[longest] + 1) % array.shape[longest]] + index_at[longest + 1:]
    return array.at[tuple(index_at)].set(least).at[tuple(next_to)].set(largest)


def setup_inputs(seed: int = 0) -> dict:
    key_of = jax.random.split(jax.random.key(seed), 4)
    return {
        "counts": draw_counts(jax.random.fold_in(key_of[3], 71), 0),
        "slice_codes": plant(jax.random.randint(key_of[1], (ORIENT, ROWS, MCOLS), 0, 2048), jax.random.fold_in(key_of[1], 1), 0, 2047).astype(jnp.int32),
        "pixel_mask": plant((jax.random.randint(key_of[2], (ROWS, MCOLS), 0, 16) < 15).astype(jnp.int32), jax.random.fold_in(key_of[2], 1), 0, 1),
    }


TIME_STEP = 0.2
EDGE_SCALE = 2.0
LOG_FLOOR = -7.0
CODE_STEP = 1.0 / 256.0

def conduct(difference):
    ratio = difference / EDGE_SCALE
    return difference / (1.0 + ratio * ratio)

def diffuse(frames):
    intensity = frames.astype(jnp.float32)
    for sweep_index in range(PASSES):
        padded = jnp.pad(intensity, ((0, 0), (1, 1), (1, 1)))
        centre = padded[:, 1:-1, 1:-1]
        flux_sum = conduct(padded[:, :-2, 1:-1] - centre) + conduct(padded[:, 2:, 1:-1] - centre)
        flux_sum = flux_sum + conduct(padded[:, 1:-1, :-2] - centre) + conduct(padded[:, 1:-1, 2:] - centre)
        intensity = centre + TIME_STEP * flux_sum
    return intensity.astype(jnp.bfloat16)

def reference(counts, slice_codes, pixel_mask):
    blocks = counts.reshape(FRAMES // FR_DEV, FR_DEV, ROWS, MCOLS)
    cleaned = lax.map(diffuse, blocks).reshape(FRAMES, ROWS * MCOLS)
    weights = pixel_mask.reshape(ROWS * MCOLS)
    masked = cleaned * weights.astype(jnp.bfloat16)[None, :]
    mask_float = weights.astype(jnp.float32)
    block_size = ORIENT // N_ORI

    def orient_block(codes):
        log_slices = (LOG_FLOOR + codes.astype(jnp.float32) * CODE_STEP).astype(jnp.bfloat16)
        log_slices = log_slices.reshape(block_size, ROWS * MCOLS)
        totals = lax.optimization_barrier(jnp.sum(jnp.exp(log_slices.astype(jnp.float32)) * mask_float[None, :], axis=1))
        cross_terms = jnp.dot(masked, log_slices.T, preferred_element_type=jnp.float32)
        return cross_terms - totals[None, :]
    parts = lax.map(orient_block, slice_codes.reshape(N_ORI, block_size, ROWS, MCOLS))
    scores = jnp.transpose(parts, (1, 0, 2)).reshape(FRAMES, ORIENT) * (1.0 / math.sqrt(ROWS * MCOLS))
    peaks = lax.optimization_barrier(jnp.max(scores, axis=1, keepdims=True))
    masses = lax.optimization_barrier(jnp.sum(jnp.exp(scores - peaks), axis=1, keepdims=True))
    log_posterior = scores - (peaks + jnp.log(masses))
    return log_posterior.reshape(N_FRM, FRAMES // N_FRM, ORIENT)
```

```python
import functools
import math

import jax
import jax.numpy as jnp
from jax import lax
from jax.experimental import pallas as pl
from jax.experimental.pallas import tpu as pltpu
from jax.sharding import PartitionSpec as P

PASSES = 8
TIME_STEP = 0.2
EDGE_SCALE = 2.0
LOG_FLOOR = -7.0
CODE_STEP = 1.0 / 256.0
GROUPS = 2
SLICE_CHUNK = 128
MESH = pl.DeviceIdType.MESH


def conduct(d):
    ratio = d * (1.0 / EDGE_SCALE)
    return d / (1.0 + ratio * ratio)


def conduct_pair(a, b):
    ra = a * (1.0 / EDGE_SCALE)
    rb = b * (1.0 / EDGE_SCALE)
    da = 1.0 + ra * ra
    db = 1.0 + rb * rb
    return (a * db + b * da) / (da * db)


def flip(h, b):
    return h + b - 2 * b * lax.rem(h // b, 2)


def kernel(
    dims, counts, codes, mask, out,
    codes_v, logs, inten, halo_s, halo_r, band_s, frames, cross, xrecv, zrecv,
    stat_s, stat_r, totals,
    code_sem, hs_sem, hr_sem, own_sem, gs_sem, gr_sem, xs_sem, xr_sem, zs_sem, zr_sem,
    ts_sem, tr_sem,
):
    nm, nf, no, fr, rows, orient, band = dims
    m, f, o = lax.axis_index("mod"), lax.axis_index("frm"), lax.axis_index("ori")
    sizes = {"mod": (m, nm), "frm": (f, nf), "ori": (o, no)}
    lanes = counts.shape[1]
    depth = band * lanes
    high = rows + 2 * PASSES
    gsz = fr // GROUPS
    group = no * fr
    share = group // nm
    chunks = orient // SLICE_CHUNK

    def other(axis, d):
        me, n = sizes[axis]
        return lax.rem(me + d, n)

    def code_copy(c):
        span = SLICE_CHUNK * band
        at = pl.ds(c * span, span)
        return pltpu.make_async_copy(codes.at[at], codes_v.at[at], code_sem.at[c])

    for c in range(chunks):
        code_copy(c).start()

    barrier = pltpu.get_barrier_semaphore()
    for axis in ("mod", "frm", "ori"):
        for d in range(1, sizes[axis][1]):
            pl.semaphore_signal(
                barrier, inc=1, device_id={axis: other(axis, d)}, device_id_type=MESH
            )

    def load_row(i, carry):
        inten[PASSES + i] = counts[pl.ds(i, fr, stride=rows), :].astype(jnp.float32)
        return carry

    lax.fori_loop(0, rows, load_row, 0)
    for i in range(PASSES):
        halo_s[0, i] = inten[PASSES + i].astype(jnp.bfloat16)
        halo_s[1, i] = inten[rows + i].astype(jnp.bfloat16)
    pl.semaphore_wait(barrier, nm + nf + no - 3)

    def halo_copy(side):
        return pltpu.make_async_remote_copy(
            src_ref=halo_s.at[side],
            dst_ref=halo_r.at[1 - side],
            send_sem=hs_sem.at[side],
            recv_sem=hr_sem.at[1 - side],
            device_id={"mod": other("mod", nm - 1 if side == 0 else 1)},
            device_id_type=MESH,
        )

    first, last = m == 0, m == nm - 1

    @pl.when(jnp.logical_not(first))
    def _():
        halo_copy(0).start()

    @pl.when(jnp.logical_not(last))
    def _():
        halo_copy(1).start()

    def slice_chunk(c):
        code_copy(c).wait()
        base = c * (SLICE_CHUNK * band)
        acc = jnp.zeros((SLICE_CHUNK, lanes), jnp.float32)
        for s in range(band):
            raw = codes_v[pl.ds(base + s, SLICE_CHUNK, stride=band), :]
            value = (LOG_FLOOR + raw.astype(jnp.float32) * CODE_STEP).astype(jnp.bfloat16)
            logs[pl.ds(c * SLICE_CHUNK, SLICE_CHUNK), pl.ds(s * lanes, lanes)] = value
            weight = mask[pl.ds(f * band + s, 1), :].astype(jnp.float32)
            acc = acc + jnp.exp(value.astype(jnp.float32)) * weight
        totals[:, pl.ds(c * SLICE_CHUNK, SLICE_CHUNK)] = jnp.sum(acc.T, axis=0, keepdims=True)

    early = chunks // 2
    for c in range(early):
        slice_chunk(c)

    @pl.when(first)
    def _():
        inten[pl.ds(0, PASSES)] = jnp.zeros((PASSES, fr, lanes), jnp.float32)

    @pl.when(jnp.logical_not(first))
    def _():
        halo_copy(1).wait_recv()
        inten[pl.ds(0, PASSES)] = halo_r[0].astype(jnp.float32)
        halo_copy(0).wait_send()

    @pl.when(last)
    def _():
        inten[pl.ds(PASSES + rows, PASSES)] = jnp.zeros((PASSES, fr, lanes), jnp.float32)

    @pl.when(jnp.logical_not(last))
    def _():
        halo_copy(0).wait_recv()
        inten[pl.ds(PASSES + rows, PASSES)] = halo_r[1].astype(jnp.float32)
        halo_copy(1).wait_send()

    lane = lax.broadcasted_iota(jnp.int32, (gsz, lanes), 1)
    at_left, at_right = lane == 0, lane == lanes - 1
    row_min = jnp.where(first, PASSES, 0)
    row_max = jnp.where(last, PASSES + rows, high)

    def diffuse(g):
        part = pl.ds(g * gsz, gsz)

        def one_row(i, c, before):
            below = inten[i + 1, part, :]
            after = conduct(below - c)
            left = jnp.where(at_left, 0.0, pltpu.roll(c, 1, 1))
            right = jnp.where(at_right, 0.0, pltpu.roll(c, lanes - 1, 1))
            side = conduct_pair(left - c, right - c)
            step = jnp.where(jnp.logical_and(i >= row_min, i < row_max), TIME_STEP, 0.0)
            inten[i, part, :] = c + step * ((after - before) + side)
            return below, after

        def one_pass(p, carry):
            centre = inten[p + 1, part, :]
            before = conduct(centre - inten[p, part, :])

            def two_rows(k, state):
                i = p + 1 + 2 * k
                c, b = one_row(i, *state)
                return one_row(i + 1, c, b)

            lax.fori_loop(0, high // 2 - 1 - p, two_rows, (centre, before))
            return carry

        lax.fori_loop(0, PASSES, one_pass, 0)
        for i in range(rows):
            good = mask[i : i + 1, :].astype(jnp.float32)
            band_s[
                pl.ds((i // band) * fr + g * gsz, gsz), pl.ds((i % band) * lanes, lanes)
            ] = (inten[PASSES + i, part, :] * good).astype(jnp.bfloat16)

    def slot(ff, oo, g):
        return frames.at[pl.ds((ff * no + oo) * fr + g * gsz, gsz)]

    pending = []
    count = [0]

    def arrived(ff, oo, g):
        pltpu.make_async_remote_copy(
            src_ref=slot(ff, oo, g), dst_ref=slot(ff, oo, g),
            send_sem=gs_sem.at[0], recv_sem=gr_sem.at[ff * no + oo, g],
            device_id={"ori": other("ori", 1)}, device_id_type=MESH,
        ).wait_recv()

    def send(src, ff, oo, g, target):
        copy = pltpu.make_async_remote_copy(
            src_ref=src, dst_ref=slot(ff, oo, g),
            send_sem=gs_sem.at[count[0]], recv_sem=gr_sem.at[ff * no + oo, g],
            device_id=target, device_id_type=MESH,
        )
        count[0] += 1
        copy.start()
        pending.append(copy)

    def banded(ff, g):
        return band_s.at[pl.ds(ff * fr + g * gsz, gsz)]

    bits = []
    b = no // 2
    while b >= 1:
        bits.append(b)
        b //= 2

    own_copies = []
    for g in range(GROUPS):
        diffuse(g)
        for d in range(1, nf):
            fd = other("frm", d)
            send(banded(fd, g), f, o, g, {"frm": fd})
        own = pltpu.make_async_copy(banded(f, g), slot(f, o, g), own_sem.at[g])
        own.start()
        own_copies.append(own)
        send(banded(f, g), f, o, g, {"ori": flip(o, bits[0])})

    todo = list(range(early, chunks))

    def some_slices(n):
        for _ in range(min(n, len(todo))):
            slice_chunk(todo.pop(0))

    for g in range(GROUPS):
        for d in range(1, nf):
            fd = other("frm", d)
            arrived(fd, o, g)
            send(slot(fd, o, g), fd, o, g, {"ori": flip(o, bits[0])})
        some_slices(1)
    some_slices(chunks)
    for own in own_copies:
        own.wait()
    held = [o]
    for k, b in enumerate(bits):
        gained = [flip(h, b) for h in held]
        if k > 0:
            for g in range(GROUPS):
                for d in range(nf):
                    for h in held:
                        send(slot(other("frm", d), h, g), other("frm", d), h, g, {"ori": flip(o, b)})
        nxt = bits[k + 1] if k + 1 < len(bits) else None
        for d in range(nf):
            for g in range(GROUPS):
                for h in gained:
                    arrived(other("frm", d), h, g)
        held = held + gained

    tile = 256
    order = [(nm // 2 + j) % nm for j in range(nm)]
    order = [q for q in order if q != 0] + [0]

    def multiply(ff):
        start = pl.multiple_of(ff * group, group)

        def one_tile(t, carry):
            at = pl.multiple_of(t * tile, tile)
            cross[pl.ds(start, group), pl.ds(at, tile)] = (
                lax.dot_general(
                    frames[pl.ds(start, group), :],
                    logs[pl.ds(at, tile), :],
                    (((1,), (1,)), ((), ())),
                    preferred_element_type=jnp.float32,
                )
                - totals[:, pl.ds(at, tile)]
            )
            return carry

        lax.fori_loop(0, orient // tile, one_tile, 0)

    def part_of(ref, ff, mm):
        return ref.at[pl.ds(ff * group + mm * share, share)]

    def x_copy(src_f, dst_f, mm, n):
        return pltpu.make_async_remote_copy(
            src_ref=part_of(cross, dst_f, mm), dst_ref=part_of(xrecv, src_f, mm),
            send_sem=xs_sem.at[n], recv_sem=xr_sem.at[src_f, mm],
            device_id={"frm": dst_f}, device_id_type=MESH,
        )

    n = 0
    for d in range(1, nf):
        fd = other("frm", d)
        multiply(fd)
        for q in order:
            copy = x_copy(f, fd, other("mod", q), n)
            copy.start()
            pending.append(copy)
            n += 1
    multiply(f)

    def z_copy(src_m, dst_m, n):
        return pltpu.make_async_remote_copy(
            src_ref=part_of(cross, f, dst_m), dst_ref=zrecv.at[src_m],
            send_sem=zs_sem.at[n], recv_sem=zr_sem.at[src_m],
            device_id={"mod": dst_m}, device_id_type=MESH,
        )

    score = None
    for k, q in enumerate(order):
        mm = other("mod", q)
        at = pl.ds(pl.multiple_of(f * group + mm * share, share), share)
        value = cross[at, :]
        for d in range(1, nf):
            fd = other("frm", d)
            x_copy(fd, other("frm", 1), mm, 0).wait_recv()
            value = value + xrecv[pl.ds(pl.multiple_of(fd * group + mm * share, share), share), :]
        if q == 0:
            score = value
        else:
            cross[at, :] = value
            copy = z_copy(m, mm, k)
            copy.start()
            pending.append(copy)
    for q in order[:-1]:
        mm = other("mod", q)
        z_copy(mm, mm, 0).wait_recv()
        score = score + zrecv[mm]
    score = score * (1.0 / math.sqrt(rows * nm * lanes))
    peak = jnp.max(score, axis=1, keepdims=True)
    mass = jnp.sum(jnp.exp(score - peak), axis=1, keepdims=True)
    wide = lax.broadcasted_iota(jnp.int32, (share, 128), 1)
    stat_s[...] = jnp.where(wide < 64, peak, mass)

    def t_copy(src_o, dst_o, n):
        return pltpu.make_async_remote_copy(
            src_ref=stat_s, dst_ref=stat_r.at[src_o],
            send_sem=ts_sem.at[n], recv_sem=tr_sem.at[src_o],
            device_id={"ori": dst_o}, device_id_type=MESH,
        )

    for d in range(1, no):
        copy = t_copy(o, other("ori", d), d)
        copy.start()
        pending.append(copy)
    peaks, masses = [peak], [mass]
    for d in range(1, no):
        od = other("ori", d)
        t_copy(od, od, 0).wait_recv()
        got = stat_r[od]
        peaks.append(got[:, 0:1])
        masses.append(got[:, 64:65])
    top = functools.reduce(jnp.maximum, peaks)
    weight = sum(s * jnp.exp(p - top) for p, s in zip(peaks, masses))
    out[...] = score - (top + jnp.log(weight))
    for copy in pending:
        copy.wait_send()


def body(counts, slice_codes, pixel_mask):
    nm, nf, no = (lax.axis_size(a) for a in ("mod", "frm", "ori"))
    fr, rows, lanes = counts.shape
    orient, band, _ = slice_codes.shape
    group = no * fr
    share = group // nm
    depth = band * lanes
    high = rows + 2 * PASSES
    dims = (nm, nf, no, fr, rows, orient, band)
    dma = pltpu.SemaphoreType.DMA
    f32, bf16 = jnp.float32, jnp.bfloat16
    vmem = pl.BlockSpec(memory_space=pltpu.VMEM)
    result = pl.pallas_call(
        functools.partial(kernel, dims),
        out_shape=jax.ShapeDtypeStruct((share, orient), f32),
        in_specs=[vmem, pl.BlockSpec(memory_space=pl.ANY), vmem],
        out_specs=vmem,
        scratch_shapes=[
            pltpu.VMEM((orient * band, lanes), jnp.int32),
            pltpu.VMEM((orient, depth), bf16),
            pltpu.VMEM((high, fr, lanes), f32),
            pltpu.VMEM((2, PASSES, fr, lanes), bf16),
            pltpu.VMEM((2, PASSES, fr, lanes), bf16),
            pltpu.VMEM((nf * fr, depth), bf16),
            pltpu.VMEM((nf * group, depth), bf16),
            pltpu.VMEM((nf * group, orient), f32),
            pltpu.VMEM((nf * group, orient), f32),
            pltpu.VMEM((nm, share, orient), f32),
            pltpu.VMEM((share, 128), f32),
            pltpu.VMEM((no, share, 128), f32),
            pltpu.VMEM((1, orient), f32),
            dma((orient // SLICE_CHUNK,)),
            dma((2,)),
            dma((2,)),
            dma((GROUPS,)),
            dma((GROUPS * nf * (no + 1),)),
            dma((nf * no, GROUPS)),
            dma((nf * nm,)),
            dma((nf, nm)),
            dma((nm,)),
            dma((nm,)),
            dma((no,)),
            dma((no,)),
        ],
        compiler_params=pltpu.CompilerParams(collective_id=0, has_side_effects=True),
    )(counts.reshape(fr * rows, lanes), slice_codes.reshape(orient * band, lanes), pixel_mask)
    return result[None]


def solution(mesh):
    in_specs = (P(("frm", "ori"), "mod", None), P("ori", ("mod", "frm"), None), P("mod", None))
    out_specs = P("frm", "mod", "ori")
    return jax.shard_map(body, mesh=mesh, in_specs=in_specs, out_specs=out_specs, check_vma=False)
```

```python
import functools
import math

import jax
import jax.numpy as jnp
from jax import lax
from jax.experimental import pallas as pl
from jax.experimental.pallas import tpu as pltpu
from jax.sharding import PartitionSpec as P

PASSES = 8
TIME_STEP = 0.2
EDGE_SCALE = 2.0
LOG_FLOOR = -7.0
CODE_STEP = 1.0 / 256.0
GROUPS = 4
STRIDE_ROWS = 8
SLICE_CHUNK = 128
MESH = pl.DeviceIdType.MESH


SQUARE = EDGE_SCALE * EDGE_SCALE


def conduct(d):
    return d / (SQUARE + d * d)


def conduct_pair(a, b):
    return (a + b) * (SQUARE + a * b) / ((SQUARE + a * a) * (SQUARE + b * b))


def flip(h, b):
    return h + b - 2 * b * lax.rem(h // b, 2)


def kernel(
    dims, counts, codes, mask, out,
    codes_v, logs, inten, halo_s, halo_r, band_s, frames, cross, xrecv, zrecv,
    stat_s, stat_r, totals,
    code_sem, hs_sem, hr_sem, own_sem, gs_sem, gr_sem, xs_sem, xr_sem, zs_sem, zr_sem,
    ts_sem, tr_sem,
):
    nm, nf, no, fr, rows, orient, band = dims
    m, f, o = lax.axis_index("mod"), lax.axis_index("frm"), lax.axis_index("ori")
    sizes = {"mod": (m, nm), "frm": (f, nf), "ori": (o, no)}
    lanes = counts.shape[1]
    depth = band * lanes
    high = rows + 2 * PASSES
    gsz = fr // GROUPS
    group = no * fr
    share = group // nm
    chunks = orient // SLICE_CHUNK

    def other(axis, d):
        me, n = sizes[axis]
        return lax.rem(me + d, n)

    def code_copy(c):
        span = SLICE_CHUNK * band
        at = pl.ds(c * span, span)
        return pltpu.make_async_copy(codes.at[at], codes_v.at[at], code_sem.at[c])

    for c in range(chunks):
        code_copy(c).start()

    barrier = pltpu.get_barrier_semaphore()
    for axis in ("mod", "frm", "ori"):
        for d in range(1, sizes[axis][1]):
            pl.semaphore_signal(
                barrier, inc=1, device_id={axis: other(axis, d)}, device_id_type=MESH
            )

    def load_row(i, carry):
        inten[PASSES + i] = counts[pl.ds(i, fr, stride=rows), :].astype(jnp.float32)
        return carry

    lax.fori_loop(0, rows, load_row, 0)
    inten[pl.ds(high, STRIDE_ROWS)] = jnp.zeros((STRIDE_ROWS, fr, lanes), jnp.float32)
    for i in range(PASSES):
        halo_s[0, i] = inten[PASSES + i].astype(jnp.bfloat16)
        halo_s[1, i] = inten[rows + i].astype(jnp.bfloat16)
    pl.semaphore_wait(barrier, nm + nf + no - 3)

    def halo_copy(side):
        return pltpu.make_async_remote_copy(
            src_ref=halo_s.at[side],
            dst_ref=halo_r.at[1 - side],
            send_sem=hs_sem.at[side],
            recv_sem=hr_sem.at[1 - side],
            device_id={"mod": other("mod", nm - 1 if side == 0 else 1)},
            device_id_type=MESH,
        )

    first, last = m == 0, m == nm - 1

    @pl.when(jnp.logical_not(first))
    def _():
        halo_copy(0).start()

    @pl.when(jnp.logical_not(last))
    def _():
        halo_copy(1).start()

    def slice_chunk(c):
        code_copy(c).wait()
        base = c * (SLICE_CHUNK * band)
        acc = jnp.zeros((SLICE_CHUNK, lanes), jnp.float32)
        for s in range(band):
            raw = codes_v[pl.ds(base + s, SLICE_CHUNK, stride=band), :]
            value = (LOG_FLOOR + raw.astype(jnp.float32) * CODE_STEP).astype(jnp.bfloat16)
            logs[pl.ds(c * SLICE_CHUNK, SLICE_CHUNK), pl.ds(s * lanes, lanes)] = value
            weight = mask[pl.ds(f * band + s, 1), :].astype(jnp.float32)
            acc = acc + jnp.exp(value.astype(jnp.float32)) * weight
        totals[:, pl.ds(c * SLICE_CHUNK, SLICE_CHUNK)] = jnp.sum(acc.T, axis=0, keepdims=True)

    early = chunks // 2
    for c in range(early):
        slice_chunk(c)

    @pl.when(first)
    def _():
        inten[pl.ds(0, PASSES)] = jnp.zeros((PASSES, fr, lanes), jnp.float32)

    @pl.when(jnp.logical_not(first))
    def _():
        halo_copy(1).wait_recv()
        inten[pl.ds(0, PASSES)] = halo_r[0].astype(jnp.float32)
        halo_copy(0).wait_send()

    @pl.when(last)
    def _():
        inten[pl.ds(PASSES + rows, PASSES)] = jnp.zeros((PASSES, fr, lanes), jnp.float32)

    @pl.when(jnp.logical_not(last))
    def _():
        halo_copy(0).wait_recv()
        inten[pl.ds(PASSES + rows, PASSES)] = halo_r[1].astype(jnp.float32)
        halo_copy(1).wait_send()

    lane = lax.broadcasted_iota(jnp.int32, (gsz, lanes), 1)
    at_left, at_right = lane == 0, lane == lanes - 1
    row_min = jnp.where(first, PASSES, 0)
    row_max = jnp.where(last, PASSES + rows, high)

    def diffuse(g):
        part = pl.ds(g * gsz, gsz)

        def one_pass(p, carry):
            centre = inten[p + 1, part, :]
            before = conduct(centre - inten[p, part, :])

            def some_rows(k, state):
                c, before = state
                i = p + 1 + STRIDE_ROWS * k
                below = [inten[i + r + 1, part, :] for r in range(STRIDE_ROWS)]
                fresh = []
                for r in range(STRIDE_ROWS):
                    after = conduct(below[r] - c)
                    left = jnp.where(at_left, 0.0, pltpu.roll(c, 1, 1))
                    right = jnp.where(at_right, 0.0, pltpu.roll(c, lanes - 1, 1))
                    side = conduct_pair(left - c, right - c)
                    inside = jnp.logical_and(i + r >= row_min, i + r < row_max)
                    step = jnp.where(inside, TIME_STEP * SQUARE, 0.0)
                    fresh.append(c + step * ((after - before) + side))
                    c, before = below[r], after
                for r in range(STRIDE_ROWS):
                    inten[i + r, part, :] = fresh[r]
                return c, before

            trips = (high - 2 * p - 3 + STRIDE_ROWS) // STRIDE_ROWS
            lax.fori_loop(0, trips, some_rows, (centre, before))
            return carry

        lax.fori_loop(0, PASSES, one_pass, 0)
        for i in range(rows):
            good = mask[i : i + 1, :].astype(jnp.float32)
            band_s[
                pl.ds((i // band) * fr + g * gsz, gsz), pl.ds((i % band) * lanes, lanes)
            ] = (inten[PASSES + i, part, :] * good).astype(jnp.bfloat16)

    def slot(ff, oo, g):
        return frames.at[pl.ds((ff * no + oo) * fr + g * gsz, gsz)]

    pending = []
    count = [0]

    def arrived(ff, oo, g):
        pltpu.make_async_remote_copy(
            src_ref=slot(ff, oo, g), dst_ref=slot(ff, oo, g),
            send_sem=gs_sem.at[0], recv_sem=gr_sem.at[ff * no + oo, g],
            device_id={"ori": other("ori", 1)}, device_id_type=MESH,
        ).wait_recv()

    def send(src, ff, oo, g, target):
        copy = pltpu.make_async_remote_copy(
            src_ref=src, dst_ref=slot(ff, oo, g),
            send_sem=gs_sem.at[count[0]], recv_sem=gr_sem.at[ff * no + oo, g],
            device_id=target, device_id_type=MESH,
        )
        count[0] += 1
        copy.start()
        pending.append(copy)

    def banded(ff, g):
        return band_s.at[pl.ds(ff * fr + g * gsz, gsz)]

    bits = []
    b = no // 2
    while b >= 1:
        bits.append(b)
        b //= 2

    held = [[o]]
    for b in bits:
        held.append(held[-1] + [flip(h, b) for h in held[-1]])

    def first_hop(g):
        for d in range(1, nf):
            fd = other("frm", d)
            send(banded(fd, g), f, o, g, {"frm": fd})
        own = pltpu.make_async_copy(banded(f, g), slot(f, o, g), own_sem.at[g])
        own.start()
        send(banded(f, g), f, o, g, {"ori": flip(o, bits[0])})
        own.wait()

    def second_hop(g):
        for d in range(1, nf):
            fd = other("frm", d)
            arrived(fd, o, g)
            send(slot(fd, o, g), fd, o, g, {"ori": flip(o, bits[0])})

    def take(k, g):
        for d in range(nf):
            for h in held[k][len(held[k]) // 2 :]:
                arrived(other("frm", d), h, g)

    def later_hop(k, g):
        take(k, g)
        if k < len(bits):
            for d in range(nf):
                for h in held[k]:
                    send(slot(other("frm", d), h, g), other("frm", d), h, g, {"ori": flip(o, bits[k])})

    hops = len(bits)
    for step in range(GROUPS):
        diffuse(step)
        first_hop(step)
        if step >= 1:
            second_hop(step - 1)
        if step >= 2:
            later_hop(1, step - 2)
    for c in range(early, early + (chunks - early + 1) // 2):
        slice_chunk(c)
    second_hop(GROUPS - 1)
    later_hop(1, GROUPS - 2)
    for c in range(early + (chunks - early + 1) // 2, chunks):
        slice_chunk(c)
    later_hop(1, GROUPS - 1)
    for k in range(2, hops + 1):
        for g in range(GROUPS):
            later_hop(k, g)

    tile = 256
    order = list(range(nm - 1, -1, -1))

    def target(q):
        mm, b = m, 1
        while b < nm:
            mm = flip(mm, b) if q & b else mm
            b *= 2
        return mm

    def multiply(ff):
        start = pl.multiple_of(ff * group, group)

        def one_tile(t, carry):
            at = pl.multiple_of(t * tile, tile)
            cross[pl.ds(start, group), pl.ds(at, tile)] = (
                lax.dot_general(
                    frames[pl.ds(start, group), :],
                    logs[pl.ds(at, tile), :],
                    (((1,), (1,)), ((), ())),
                    preferred_element_type=jnp.float32,
                )
                - totals[:, pl.ds(at, tile)]
            )
            return carry

        lax.fori_loop(0, orient // tile, one_tile, 0)

    def part_of(ref, ff, mm):
        return ref.at[pl.ds(ff * group + mm * share, share)]

    def x_copy(src_f, dst_f, mm, n):
        return pltpu.make_async_remote_copy(
            src_ref=part_of(cross, dst_f, mm), dst_ref=part_of(xrecv, src_f, mm),
            send_sem=xs_sem.at[n], recv_sem=xr_sem.at[src_f, mm],
            device_id={"frm": dst_f}, device_id_type=MESH,
        )

    n = 0
    for d in range(1, nf):
        fd = other("frm", d)
        multiply(fd)
        for q in order:
            copy = x_copy(f, fd, target(q), n)
            copy.start()
            pending.append(copy)
            n += 1
    multiply(f)

    def z_copy(q):
        return pltpu.make_async_remote_copy(
            src_ref=part_of(cross, f, target(q)), dst_ref=zrecv.at[q],
            send_sem=zs_sem.at[q], recv_sem=zr_sem.at[q],
            device_id={"mod": flip(m, q & -q)}, device_id_type=MESH,
        )

    score = None
    for q in order:
        mm = target(q)
        at = pl.ds(pl.multiple_of(f * group + mm * share, share), share)
        value = cross[at, :]
        for d in range(1, nf):
            fd = other("frm", d)
            x_copy(fd, other("frm", 1), mm, 0).wait_recv()
            value = value + xrecv[pl.ds(pl.multiple_of(fd * group + mm * share, share), share), :]
        b = 1
        while b < nm and not q & b:
            z_copy(q | b).wait_recv()
            value = value + zrecv[q | b]
            b *= 2
        if q == 0:
            score = value
        else:
            cross[at, :] = value
            copy = z_copy(q)
            copy.start()
            pending.append(copy)
    score = score * (1.0 / math.sqrt(rows * nm * lanes))
    peak = jnp.max(score, axis=1, keepdims=True)
    mass = jnp.sum(jnp.exp(score - peak), axis=1, keepdims=True)
    wide = lax.broadcasted_iota(jnp.int32, (share, 128), 1)
    stat_s[...] = jnp.where(wide < 64, peak, mass)

    def t_copy(src_o, dst_o, n):
        return pltpu.make_async_remote_copy(
            src_ref=stat_s, dst_ref=stat_r.at[src_o],
            send_sem=ts_sem.at[n], recv_sem=tr_sem.at[src_o],
            device_id={"ori": dst_o}, device_id_type=MESH,
        )

    for d in range(1, no):
        copy = t_copy(o, other("ori", d), d)
        copy.start()
        pending.append(copy)
    peaks, masses = [peak], [mass]
    for d in range(1, no):
        od = other("ori", d)
        t_copy(od, od, 0).wait_recv()
        got = stat_r[od]
        peaks.append(got[:, 0:1])
        masses.append(got[:, 64:65])
    top = functools.reduce(jnp.maximum, peaks)
    weight = sum(s * jnp.exp(p - top) for p, s in zip(peaks, masses))
    out[...] = score - (top + jnp.log(weight))
    for copy in pending:
        copy.wait_send()


def body(counts, slice_codes, pixel_mask):
    nm, nf, no = (lax.axis_size(a) for a in ("mod", "frm", "ori"))
    fr, rows, lanes = counts.shape
    orient, band, _ = slice_codes.shape
    group = no * fr
    share = group // nm
    depth = band * lanes
    high = rows + 2 * PASSES
    dims = (nm, nf, no, fr, rows, orient, band)
    dma = pltpu.SemaphoreType.DMA
    f32, bf16 = jnp.float32, jnp.bfloat16
    vmem = pl.BlockSpec(memory_space=pltpu.VMEM)
    result = pl.pallas_call(
        functools.partial(kernel, dims),
        out_shape=jax.ShapeDtypeStruct((share, orient), f32),
        in_specs=[vmem, pl.BlockSpec(memory_space=pl.ANY), vmem],
        out_specs=vmem,
        scratch_shapes=[
            pltpu.VMEM((orient * band, lanes), jnp.int32),
            pltpu.VMEM((orient, depth), bf16),
            pltpu.VMEM((high + STRIDE_ROWS, fr, lanes), f32),
            pltpu.VMEM((2, PASSES, fr, lanes), bf16),
            pltpu.VMEM((2, PASSES, fr, lanes), bf16),
            pltpu.VMEM((nf * fr, depth), bf16),
            pltpu.VMEM((nf * group, depth), bf16),
            pltpu.VMEM((nf * group, orient), f32),
            pltpu.VMEM((nf * group, orient), f32),
            pltpu.VMEM((nm, share, orient), f32),
            pltpu.VMEM((share, 128), f32),
            pltpu.VMEM((no, share, 128), f32),
            pltpu.VMEM((1, orient), f32),
            dma((orient // SLICE_CHUNK,)),
            dma((2,)),
            dma((2,)),
            dma((GROUPS,)),
            dma((GROUPS * nf * (no + 1),)),
            dma((nf * no, GROUPS)),
            dma((nf * nm,)),
            dma((nf, nm)),
            dma((nm,)),
            dma((nm,)),
            dma((no,)),
            dma((no,)),
        ],
        compiler_params=pltpu.CompilerParams(collective_id=0, has_side_effects=True),
    )(counts.reshape(fr * rows, lanes), slice_codes.reshape(orient * band, lanes), pixel_mask)
    return result[None]


def solution(mesh):
    in_specs = (P(("frm", "ori"), "mod", None), P("ori", ("mod", "frm"), None), P("mod", None))
    out_specs = P("frm", "mod", "ori")
    return jax.shard_map(body, mesh=mesh, in_specs=in_specs, out_specs=out_specs, check_vma=False)
```

```python
import functools
import math

import jax
import jax.numpy as jnp
from jax import lax
from jax.experimental import pallas as pl
from jax.experimental.pallas import tpu as pltpu
from jax.sharding import PartitionSpec as P

PASSES = 8
TIME_STEP = 0.2
EDGE_SCALE = 2.0
LOG_FLOOR = -7.0
CODE_STEP = 1.0 / 256.0
GROUPS = 4
STRIDE_ROWS = 8
SLICE_CHUNK = 128
MESH = pl.DeviceIdType.MESH


SQUARE = EDGE_SCALE * EDGE_SCALE


def conduct(d):
    return d / (SQUARE + d * d)


def conduct_pair(a, b):
    return (a + b) * (SQUARE + a * b) / ((SQUARE + a * a) * (SQUARE + b * b))


def flip(h, b):
    return h + b - 2 * b * lax.rem(h // b, 2)


def kernel(
    dims, counts, codes, mask, out,
    codes_v, logs, inten, halo_s, halo_r, band_s, frames, early_part, cross, xrecv, zrecv,
    stat_s, stat_r, totals,
    code_sem, hs_sem, hr_sem, own_sem, gs_sem, gr_sem, xs_sem, xr_sem, zs_sem, zr_sem,
    ts_sem, tr_sem,
):
    nm, nf, no, fr, rows, orient, band = dims
    m, f, o = lax.axis_index("mod"), lax.axis_index("frm"), lax.axis_index("ori")
    sizes = {"mod": (m, nm), "frm": (f, nf), "ori": (o, no)}
    lanes = counts.shape[1]
    depth = band * lanes
    high = rows + 2 * PASSES
    gsz = fr // GROUPS
    group = no * fr
    share = group // nm
    chunks = orient // SLICE_CHUNK

    def other(axis, d):
        me, n = sizes[axis]
        return lax.rem(me + d, n)

    def code_copy(c):
        span = SLICE_CHUNK * band
        at = pl.ds(c * span, span)
        return pltpu.make_async_copy(codes.at[at], codes_v.at[at], code_sem.at[c])

    for c in range(chunks):
        code_copy(c).start()

    barrier = pltpu.get_barrier_semaphore()
    for axis in ("mod", "frm", "ori"):
        for d in range(1, sizes[axis][1]):
            pl.semaphore_signal(
                barrier, inc=1, device_id={axis: other(axis, d)}, device_id_type=MESH
            )

    def load_row(i, carry):
        inten[PASSES + i] = counts[pl.ds(i, fr, stride=rows), :].astype(jnp.float32)
        return carry

    lax.fori_loop(0, rows, load_row, 0)
    inten[pl.ds(high, STRIDE_ROWS)] = jnp.zeros((STRIDE_ROWS, fr, lanes), jnp.float32)
    for i in range(PASSES):
        halo_s[0, i] = inten[PASSES + i].astype(jnp.bfloat16)
        halo_s[1, i] = inten[rows + i].astype(jnp.bfloat16)
    pl.semaphore_wait(barrier, nm + nf + no - 3)

    def halo_copy(side):
        return pltpu.make_async_remote_copy(
            src_ref=halo_s.at[side],
            dst_ref=halo_r.at[1 - side],
            send_sem=hs_sem.at[side],
            recv_sem=hr_sem.at[1 - side],
            device_id={"mod": other("mod", nm - 1 if side == 0 else 1)},
            device_id_type=MESH,
        )

    first, last = m == 0, m == nm - 1

    @pl.when(jnp.logical_not(first))
    def _():
        halo_copy(0).start()

    @pl.when(jnp.logical_not(last))
    def _():
        halo_copy(1).start()

    def slice_chunk(c):
        code_copy(c).wait()
        base = c * (SLICE_CHUNK * band)
        acc = jnp.zeros((SLICE_CHUNK, lanes), jnp.float32)
        for s in range(band):
            raw = codes_v[pl.ds(base + s, SLICE_CHUNK, stride=band), :]
            value = (LOG_FLOOR + raw.astype(jnp.float32) * CODE_STEP).astype(jnp.bfloat16)
            logs[pl.ds(c * SLICE_CHUNK, SLICE_CHUNK), pl.ds(s * lanes, lanes)] = value
            weight = mask[pl.ds(f * band + s, 1), :].astype(jnp.float32)
            acc = acc + jnp.exp(value.astype(jnp.float32)) * weight
        totals[:, pl.ds(c * SLICE_CHUNK, SLICE_CHUNK)] = jnp.sum(acc.T, axis=0, keepdims=True)

    early = chunks // 2
    for c in range(early):
        slice_chunk(c)

    @pl.when(first)
    def _():
        inten[pl.ds(0, PASSES)] = jnp.zeros((PASSES, fr, lanes), jnp.float32)

    @pl.when(jnp.logical_not(first))
    def _():
        halo_copy(1).wait_recv()
        inten[pl.ds(0, PASSES)] = halo_r[0].astype(jnp.float32)
        halo_copy(0).wait_send()

    @pl.when(last)
    def _():
        inten[pl.ds(PASSES + rows, PASSES)] = jnp.zeros((PASSES, fr, lanes), jnp.float32)

    @pl.when(jnp.logical_not(last))
    def _():
        halo_copy(0).wait_recv()
        inten[pl.ds(PASSES + rows, PASSES)] = halo_r[1].astype(jnp.float32)
        halo_copy(1).wait_send()

    lane = lax.broadcasted_iota(jnp.int32, (gsz, lanes), 1)
    at_left, at_right = lane == 0, lane == lanes - 1
    row_min = jnp.where(first, PASSES, 0)
    row_max = jnp.where(last, PASSES + rows, high)

    def diffuse(g):
        part = pl.ds(g * gsz, gsz)

        def one_pass(p, carry):
            centre = inten[p + 1, part, :]
            before = conduct(centre - inten[p, part, :])

            def some_rows(k, state):
                c, before = state
                i = p + 1 + STRIDE_ROWS * k
                below = [inten[i + r + 1, part, :] for r in range(STRIDE_ROWS)]
                fresh = []
                for r in range(STRIDE_ROWS):
                    after = conduct(below[r] - c)
                    left = jnp.where(at_left, 0.0, pltpu.roll(c, 1, 1))
                    right = jnp.where(at_right, 0.0, pltpu.roll(c, lanes - 1, 1))
                    side = conduct_pair(left - c, right - c)
                    inside = jnp.logical_and(i + r >= row_min, i + r < row_max)
                    step = jnp.where(inside, TIME_STEP * SQUARE, 0.0)
                    fresh.append(c + step * ((after - before) + side))
                    c, before = below[r], after
                for r in range(STRIDE_ROWS):
                    inten[i + r, part, :] = fresh[r]
                return c, before

            trips = (high - 2 * p - 3 + STRIDE_ROWS) // STRIDE_ROWS
            lax.fori_loop(0, trips, some_rows, (centre, before))
            return carry

        lax.fori_loop(0, PASSES, one_pass, 0)
        for i in range(rows):
            good = mask[i : i + 1, :].astype(jnp.float32)
            band_s[
                pl.ds((i // band) * fr + g * gsz, gsz), pl.ds((i % band) * lanes, lanes)
            ] = (inten[PASSES + i, part, :] * good).astype(jnp.bfloat16)

    def slot(ff, oo, g):
        return frames.at[pl.ds((ff * no + oo) * fr + g * gsz, gsz)]

    pending = []
    count = [0]

    def arrived(ff, oo, g):
        pltpu.make_async_remote_copy(
            src_ref=slot(ff, oo, g), dst_ref=slot(ff, oo, g),
            send_sem=gs_sem.at[0], recv_sem=gr_sem.at[ff * no + oo, g],
            device_id={"ori": other("ori", 1)}, device_id_type=MESH,
        ).wait_recv()

    def send(src, ff, oo, g, target):
        copy = pltpu.make_async_remote_copy(
            src_ref=src, dst_ref=slot(ff, oo, g),
            send_sem=gs_sem.at[count[0]], recv_sem=gr_sem.at[ff * no + oo, g],
            device_id=target, device_id_type=MESH,
        )
        count[0] += 1
        copy.start()
        pending.append(copy)

    def banded(ff, g):
        return band_s.at[pl.ds(ff * fr + g * gsz, gsz)]

    bits = []
    b = no // 2
    while b >= 1:
        bits.append(b)
        b //= 2

    held = [[o]]
    for b in bits:
        held.append(held[-1] + [flip(h, b) for h in held[-1]])

    def first_hop(g):
        for d in range(1, nf):
            fd = other("frm", d)
            send(banded(fd, g), f, o, g, {"frm": fd})
        own = pltpu.make_async_copy(banded(f, g), slot(f, o, g), own_sem.at[g])
        own.start()
        send(banded(f, g), f, o, g, {"ori": flip(o, bits[0])})
        own.wait()

    def second_hop(g):
        for d in range(1, nf):
            fd = other("frm", d)
            arrived(fd, o, g)
            send(slot(fd, o, g), fd, o, g, {"ori": flip(o, bits[0])})

    def take(k, g):
        for d in range(nf):
            for h in held[k][len(held[k]) // 2 :]:
                arrived(other("frm", d), h, g)

    def later_hop(k, g):
        take(k, g)
        if k < len(bits):
            for d in range(nf):
                for h in held[k]:
                    send(slot(other("frm", d), h, g), other("frm", d), h, g, {"ori": flip(o, bits[k])})

    tile = 256

    def part_of(ref, ff, mm):
        return ref.at[pl.ds(ff * group + mm * share, share)]

    per = fr // share if fr % share == 0 else 0

    def x_copy(src_f, dst_f, mm, source=None):
        return pltpu.make_async_remote_copy(
            src_ref=part_of(cross, dst_f, mm) if source is None else source,
            dst_ref=part_of(xrecv, src_f, mm),
            send_sem=xs_sem.at[dst_f, mm], recv_sem=xr_sem.at[src_f, mm],
            device_id={"frm": dst_f}, device_id_type=MESH,
        )

    def early_scores(d):
        fd = other("frm", d)
        rows_at = pl.ds(pl.multiple_of((fd * no + o) * fr, fr), fr)

        def one_tile(t, carry):
            at = pl.multiple_of(t * tile, tile)
            early_part[pl.ds((d - 1) * fr, fr), pl.ds(at, tile)] = (
                lax.dot_general(
                    frames[rows_at, :],
                    logs[pl.ds(at, tile), :],
                    (((1,), (1,)), ((), ())),
                    preferred_element_type=jnp.float32,
                )
                - totals[:, pl.ds(at, tile)]
            )
            return carry

        lax.fori_loop(0, orient // tile, one_tile, 0)
        for j in range(per):
            source = early_part.at[pl.ds((d - 1) * fr + j * share, share)]
            x_copy(f, fd, o * per + j, source).start()

    hops = len(bits)
    for step in range(GROUPS):
        diffuse(step)
        first_hop(step)
        if step >= 1:
            second_hop(step - 1)
        if step >= 2:
            later_hop(1, step - 2)
    for c in range(early, early + (chunks - early + 1) // 2):
        slice_chunk(c)
    second_hop(GROUPS - 1)
    later_hop(1, GROUPS - 2)
    for c in range(early + (chunks - early + 1) // 2, chunks):
        slice_chunk(c)
    if per:
        for d in range(1, nf):
            early_scores(d)
    later_hop(1, GROUPS - 1)
    for k in range(2, hops + 1):
        for g in range(GROUPS):
            later_hop(k, g)

    order = list(range(nm - 1, -1, -1))

    def target(q):
        mm, b = m, 1
        while b < nm:
            mm = flip(mm, b) if q & b else mm
            b *= 2
        return mm

    def multiply(ff):
        start = pl.multiple_of(ff * group, group)

        def one_tile(t, carry):
            at = pl.multiple_of(t * tile, tile)
            cross[pl.ds(start, group), pl.ds(at, tile)] = (
                lax.dot_general(
                    frames[pl.ds(start, group), :],
                    logs[pl.ds(at, tile), :],
                    (((1,), (1,)), ((), ())),
                    preferred_element_type=jnp.float32,
                )
                - totals[:, pl.ds(at, tile)]
            )
            return carry

        lax.fori_loop(0, orient // tile, one_tile, 0)

    def x_start(fd, mm):
        if not per:
            x_copy(f, fd, mm).start()
            return

        @pl.when(mm // per != o)
        def _():
            x_copy(f, fd, mm).start()

    for d in range(1, nf):
        fd = other("frm", d)
        multiply(fd)
        for q in order:
            x_start(fd, target(q))
    multiply(f)

    def z_copy(q):
        return pltpu.make_async_remote_copy(
            src_ref=part_of(cross, f, target(q)), dst_ref=zrecv.at[q],
            send_sem=zs_sem.at[q], recv_sem=zr_sem.at[q],
            device_id={"mod": flip(m, q & -q)}, device_id_type=MESH,
        )

    score = None
    for q in order:
        mm = target(q)
        at = pl.ds(pl.multiple_of(f * group + mm * share, share), share)
        value = cross[at, :]
        for d in range(1, nf):
            fd = other("frm", d)
            x_copy(fd, other("frm", 1), mm).wait_recv()
            value = value + xrecv[pl.ds(pl.multiple_of(fd * group + mm * share, share), share), :]
        b = 1
        while b < nm and not q & b:
            z_copy(q | b).wait_recv()
            value = value + zrecv[q | b]
            b *= 2
        if q == 0:
            score = value
        else:
            cross[at, :] = value
            copy = z_copy(q)
            copy.start()
            pending.append(copy)
    score = score * (1.0 / math.sqrt(rows * nm * lanes))
    peak = jnp.max(score, axis=1, keepdims=True)
    mass = jnp.sum(jnp.exp(score - peak), axis=1, keepdims=True)
    wide = lax.broadcasted_iota(jnp.int32, (share, 128), 1)
    stat_s[...] = jnp.where(wide < 64, peak, mass)

    def t_copy(src_o, dst_o, n):
        return pltpu.make_async_remote_copy(
            src_ref=stat_s, dst_ref=stat_r.at[src_o],
            send_sem=ts_sem.at[n], recv_sem=tr_sem.at[src_o],
            device_id={"ori": dst_o}, device_id_type=MESH,
        )

    for d in range(1, no):
        copy = t_copy(o, other("ori", d), d)
        copy.start()
        pending.append(copy)
    peaks, masses = [peak], [mass]
    for d in range(1, no):
        od = other("ori", d)
        t_copy(od, od, 0).wait_recv()
        got = stat_r[od]
        peaks.append(got[:, 0:1])
        masses.append(got[:, 64:65])
    top = functools.reduce(jnp.maximum, peaks)
    weight = sum(s * jnp.exp(p - top) for p, s in zip(peaks, masses))
    out[...] = score - (top + jnp.log(weight))
    for d in range(1, nf):
        for mm in range(nm):
            x_copy(f, other("frm", d), mm).wait_send()
    for copy in pending:
        copy.wait_send()


def body(counts, slice_codes, pixel_mask):
    nm, nf, no = (lax.axis_size(a) for a in ("mod", "frm", "ori"))
    fr, rows, lanes = counts.shape
    orient, band, _ = slice_codes.shape
    group = no * fr
    share = group // nm
    depth = band * lanes
    high = rows + 2 * PASSES
    dims = (nm, nf, no, fr, rows, orient, band)
    dma = pltpu.SemaphoreType.DMA
    f32, bf16 = jnp.float32, jnp.bfloat16
    vmem = pl.BlockSpec(memory_space=pltpu.VMEM)
    result = pl.pallas_call(
        functools.partial(kernel, dims),
        out_shape=jax.ShapeDtypeStruct((share, orient), f32),
        in_specs=[vmem, pl.BlockSpec(memory_space=pl.ANY), vmem],
        out_specs=vmem,
        scratch_shapes=[
            pltpu.VMEM((orient * band, lanes), jnp.int32),
            pltpu.VMEM((orient, depth), bf16),
            pltpu.VMEM((high + STRIDE_ROWS, fr, lanes), f32),
            pltpu.VMEM((2, PASSES, fr, lanes), bf16),
            pltpu.VMEM((2, PASSES, fr, lanes), bf16),
            pltpu.VMEM((nf * fr, depth), bf16),
            pltpu.VMEM((nf * group, depth), bf16),
            pltpu.VMEM((nf * fr, orient), f32),
            pltpu.VMEM((nf * group, orient), f32),
            pltpu.VMEM((nf * group, orient), f32),
            pltpu.VMEM((nm, share, orient), f32),
            pltpu.VMEM((share, 128), f32),
            pltpu.VMEM((no, share, 128), f32),
            pltpu.VMEM((1, orient), f32),
            dma((orient // SLICE_CHUNK,)),
            dma((2,)),
            dma((2,)),
            dma((GROUPS,)),
            dma((GROUPS * nf * (no + 1),)),
            dma((nf * no, GROUPS)),
            dma((nf, nm)),
            dma((nf, nm)),
            dma((nm,)),
            dma((nm,)),
            dma((no,)),
            dma((no,)),
        ],
        compiler_params=pltpu.CompilerParams(collective_id=0, has_side_effects=True),
    )(counts.reshape(fr * rows, lanes), slice_codes.reshape(orient * band, lanes), pixel_mask)
    return result[None]


def solution(mesh):
    in_specs = (P(("frm", "ori"), "mod", None), P("ori", ("mod", "frm"), None), P("mod", None))
    out_specs = P("frm", "mod", "ori")
    return jax.shard_map(body, mesh=mesh, in_specs=in_specs, out_specs=out_specs, check_vma=False)
```

```python
import functools
import math

import jax
import jax.numpy as jnp
from jax import lax
from jax.experimental import pallas as pl
from jax.experimental.pallas import tpu as pltpu
from jax.sharding import PartitionSpec as P

PASSES = 8
TIME_STEP = 0.2
EDGE_SCALE = 2.0
LOG_FLOOR = -7.0
CODE_STEP = 1.0 / 256.0
GROUPS = 2
STRIDE_ROWS = 8
SLICE_CHUNK = 128
MESH = pl.DeviceIdType.MESH


SQUARE = EDGE_SCALE * EDGE_SCALE


def conduct(d):
    return d / (SQUARE + d * d)


def conduct_pair(a, b):
    return (a + b) * (SQUARE + a * b) / ((SQUARE + a * a) * (SQUARE + b * b))


def flip(h, b):
    return h + b - 2 * b * lax.rem(h // b, 2)


def kernel(
    dims, counts, codes, mask, out,
    codes_v, logs, inten, halo_s, halo_r, band_s, frames, cross, xrecv, zrecv,
    stat_s, stat_r, totals,
    code_sem, hs_sem, hr_sem, own_sem, gs_sem, gr_sem, xs_sem, xr_sem, zs_sem, zr_sem,
    ts_sem, tr_sem,
):
    nm, nf, no, fr, rows, orient, band = dims
    m, f, o = lax.axis_index("mod"), lax.axis_index("frm"), lax.axis_index("ori")
    sizes = {"mod": (m, nm), "frm": (f, nf), "ori": (o, no)}
    lanes = counts.shape[1]
    depth = band * lanes
    high = rows + 2 * PASSES
    gsz = fr // GROUPS
    group = no * fr
    share = group // nm
    chunks = orient // SLICE_CHUNK

    def other(axis, d):
        me, n = sizes[axis]
        return lax.rem(me + d, n)

    def code_copy(c):
        span = SLICE_CHUNK * band
        at = pl.ds(c * span, span)
        return pltpu.make_async_copy(codes.at[at], codes_v.at[at], code_sem.at[c])

    for c in range(chunks):
        code_copy(c).start()

    barrier = pltpu.get_barrier_semaphore()
    for axis in ("mod", "frm", "ori"):
        for d in range(1, sizes[axis][1]):
            pl.semaphore_signal(
                barrier, inc=1, device_id={axis: other(axis, d)}, device_id_type=MESH
            )

    def load_row(i, carry):
        inten[PASSES + i] = counts[pl.ds(i, fr, stride=rows), :].astype(jnp.float32)
        return carry

    lax.fori_loop(0, rows, load_row, 0)
    inten[pl.ds(high, STRIDE_ROWS)] = jnp.zeros((STRIDE_ROWS, fr, lanes), jnp.float32)
    for i in range(PASSES):
        halo_s[0, i] = inten[PASSES + i].astype(jnp.bfloat16)
        halo_s[1, i] = inten[rows + i].astype(jnp.bfloat16)
    pl.semaphore_wait(barrier, nm + nf + no - 3)

    def halo_copy(side):
        return pltpu.make_async_remote_copy(
            src_ref=halo_s.at[side],
            dst_ref=halo_r.at[1 - side],
            send_sem=hs_sem.at[side],
            recv_sem=hr_sem.at[1 - side],
            device_id={"mod": other("mod", nm - 1 if side == 0 else 1)},
            device_id_type=MESH,
        )

    first, last = m == 0, m == nm - 1

    @pl.when(jnp.logical_not(first))
    def _():
        halo_copy(0).start()

    @pl.when(jnp.logical_not(last))
    def _():
        halo_copy(1).start()

    def slice_chunk(c):
        code_copy(c).wait()
        base = c * (SLICE_CHUNK * band)
        acc = jnp.zeros((SLICE_CHUNK, lanes), jnp.float32)
        for s in range(band):
            raw = codes_v[pl.ds(base + s, SLICE_CHUNK, stride=band), :]
            value = (LOG_FLOOR + raw.astype(jnp.float32) * CODE_STEP).astype(jnp.bfloat16)
            logs[pl.ds(c * SLICE_CHUNK, SLICE_CHUNK), pl.ds(s * lanes, lanes)] = value
            weight = mask[pl.ds(f * band + s, 1), :].astype(jnp.float32)
            acc = acc + jnp.exp(value.astype(jnp.float32)) * weight
        totals[:, pl.ds(c * SLICE_CHUNK, SLICE_CHUNK)] = jnp.sum(acc.T, axis=0, keepdims=True)

    early = chunks // 2
    for c in range(early):
        slice_chunk(c)

    @pl.when(first)
    def _():
        inten[pl.ds(0, PASSES)] = jnp.zeros((PASSES, fr, lanes), jnp.float32)

    @pl.when(jnp.logical_not(first))
    def _():
        halo_copy(1).wait_recv()
        inten[pl.ds(0, PASSES)] = halo_r[0].astype(jnp.float32)
        halo_copy(0).wait_send()

    @pl.when(last)
    def _():
        inten[pl.ds(PASSES + rows, PASSES)] = jnp.zeros((PASSES, fr, lanes), jnp.float32)

    @pl.when(jnp.logical_not(last))
    def _():
        halo_copy(0).wait_recv()
        inten[pl.ds(PASSES + rows, PASSES)] = halo_r[1].astype(jnp.float32)
        halo_copy(1).wait_send()

    lane = lax.broadcasted_iota(jnp.int32, (gsz, lanes), 1)
    at_left, at_right = lane == 0, lane == lanes - 1
    row_min = jnp.where(first, PASSES, 0)
    row_max = jnp.where(last, PASSES + rows, high)

    def diffuse(g):
        part = pl.ds(g * gsz, gsz)

        def one_pass(p, carry):
            centre = inten[p + 1, part, :]
            before = conduct(centre - inten[p, part, :])

            def some_rows(k, state):
                c, before = state
                i = p + 1 + STRIDE_ROWS * k
                below = [inten[i + r + 1, part, :] for r in range(STRIDE_ROWS)]
                fresh = []
                for r in range(STRIDE_ROWS):
                    after = conduct(below[r] - c)
                    left = jnp.where(at_left, 0.0, pltpu.roll(c, 1, 1))
                    right = jnp.where(at_right, 0.0, pltpu.roll(c, lanes - 1, 1))
                    side = conduct_pair(left - c, right - c)
                    inside = jnp.logical_and(i + r >= row_min, i + r < row_max)
                    step = jnp.where(inside, TIME_STEP * SQUARE, 0.0)
                    fresh.append(c + step * ((after - before) + side))
                    c, before = below[r], after
                for r in range(STRIDE_ROWS):
                    inten[i + r, part, :] = fresh[r]
                return c, before

            trips = (high - 2 * p - 3 + STRIDE_ROWS) // STRIDE_ROWS
            lax.fori_loop(0, trips, some_rows, (centre, before))
            return carry

        lax.fori_loop(0, PASSES, one_pass, 0)
        for i in range(rows):
            good = mask[i : i + 1, :].astype(jnp.float32)
            band_s[
                pl.ds((i // band) * fr + g * gsz, gsz), pl.ds((i % band) * lanes, lanes)
            ] = (inten[PASSES + i, part, :] * good).astype(jnp.bfloat16)

    def slot(ff, oo, g):
        return frames.at[pl.ds((ff * no + oo) * fr + g * gsz, gsz)]

    pending = []
    count = [0]

    def arrived(ff, oo, g):
        pltpu.make_async_remote_copy(
            src_ref=slot(ff, oo, g), dst_ref=slot(ff, oo, g),
            send_sem=gs_sem.at[0], recv_sem=gr_sem.at[ff * no + oo, g],
            device_id={"ori": other("ori", 1)}, device_id_type=MESH,
        ).wait_recv()

    def send(src, ff, oo, g, target):
        copy = pltpu.make_async_remote_copy(
            src_ref=src, dst_ref=slot(ff, oo, g),
            send_sem=gs_sem.at[count[0]], recv_sem=gr_sem.at[ff * no + oo, g],
            device_id=target, device_id_type=MESH,
        )
        count[0] += 1
        copy.start()
        pending.append(copy)

    def banded(ff, g):
        return band_s.at[pl.ds(ff * fr + g * gsz, gsz)]

    bits = []
    b = no // 2
    while b >= 1:
        bits.append(b)
        b //= 2

    held = [[o]]
    for b in bits:
        held.append(held[-1] + [flip(h, b) for h in held[-1]])

    def first_hop(g):
        for d in range(1, nf):
            fd = other("frm", d)
            send(banded(fd, g), f, o, g, {"frm": fd})
        own = pltpu.make_async_copy(banded(f, g), slot(f, o, g), own_sem.at[g])
        own.start()
        send(banded(f, g), f, o, g, {"ori": flip(o, bits[0])})
        own.wait()

    def second_hop(g):
        for d in range(1, nf):
            fd = other("frm", d)
            arrived(fd, o, g)
            send(slot(fd, o, g), fd, o, g, {"ori": flip(o, bits[0])})

    def take(k, g):
        for d in range(nf):
            for h in held[k][len(held[k]) // 2 :]:
                arrived(other("frm", d), h, g)

    def later_hop(k, g):
        take(k, g)
        if k < len(bits):
            for d in range(nf):
                for h in held[k]:
                    send(slot(other("frm", d), h, g), other("frm", d), h, g, {"ori": flip(o, bits[k])})

    hops = len(bits)
    for step in range(GROUPS):
        diffuse(step)
        first_hop(step)
        if step >= 1:
            second_hop(step - 1)
        if step >= 2:
            later_hop(1, step - 2)
    for c in range(early, early + (chunks - early + 1) // 2):
        slice_chunk(c)
    second_hop(GROUPS - 1)
    later_hop(1, GROUPS - 2)
    for c in range(early + (chunks - early + 1) // 2, chunks):
        slice_chunk(c)
    later_hop(1, GROUPS - 1)
    for k in range(2, hops + 1):
        for g in range(GROUPS):
            later_hop(k, g)

    tile = 256
    order = list(range(nm - 1, -1, -1))

    def target(q):
        mm, b = m, 1
        while b < nm:
            mm = flip(mm, b) if q & b else mm
            b *= 2
        return mm

    def multiply(ff):
        start = pl.multiple_of(ff * group, group)

        def one_tile(t, carry):
            at = pl.multiple_of(t * tile, tile)
            cross[pl.ds(start, group), pl.ds(at, tile)] = (
                lax.dot_general(
                    frames[pl.ds(start, group), :],
                    logs[pl.ds(at, tile), :],
                    (((1,), (1,)), ((), ())),
                    preferred_element_type=jnp.float32,
                )
                - totals[:, pl.ds(at, tile)]
            )
            return carry

        lax.fori_loop(0, orient // tile, one_tile, 0)

    def part_of(ref, ff, mm):
        return ref.at[pl.ds(ff * group + mm * share, share)]

    def x_copy(src_f, dst_f, mm, n):
        return pltpu.make_async_remote_copy(
            src_ref=part_of(cross, dst_f, mm), dst_ref=part_of(xrecv, src_f, mm),
            send_sem=xs_sem.at[n], recv_sem=xr_sem.at[src_f, mm],
            device_id={"frm": dst_f}, device_id_type=MESH,
        )

    n = 0
    for d in range(1, nf):
        fd = other("frm", d)
        multiply(fd)
        for q in order:
            copy = x_copy(f, fd, target(q), n)
            copy.start()
            pending.append(copy)
            n += 1
    multiply(f)

    def z_copy(q):
        return pltpu.make_async_remote_copy(
            src_ref=part_of(cross, f, target(q)), dst_ref=zrecv.at[q],
            send_sem=zs_sem.at[q], recv_sem=zr_sem.at[q],
            device_id={"mod": flip(m, q & -q)}, device_id_type=MESH,
        )

    score = None
    for q in order:
        mm = target(q)
        at = pl.ds(pl.multiple_of(f * group + mm * share, share), share)
        value = cross[at, :]
        for d in range(1, nf):
            fd = other("frm", d)
            x_copy(fd, other("frm", 1), mm, 0).wait_recv()
            value = value + xrecv[pl.ds(pl.multiple_of(fd * group + mm * share, share), share), :]
        b = 1
        while b < nm and not q & b:
            z_copy(q | b).wait_recv()
            value = value + zrecv[q | b]
            b *= 2
        if q == 0:
            score = value
        else:
            cross[at, :] = value
            copy = z_copy(q)
            copy.start()
            pending.append(copy)
    score = score * (1.0 / math.sqrt(rows * nm * lanes))
    peak = jnp.max(score, axis=1, keepdims=True)
    mass = jnp.sum(jnp.exp(score - peak), axis=1, keepdims=True)
    wide = lax.broadcasted_iota(jnp.int32, (share, 128), 1)
    stat_s[...] = jnp.where(wide < 64, peak, mass)

    def t_copy(src_o, dst_o, n):
        return pltpu.make_async_remote_copy(
            src_ref=stat_s, dst_ref=stat_r.at[src_o],
            send_sem=ts_sem.at[n], recv_sem=tr_sem.at[src_o],
            device_id={"ori": dst_o}, device_id_type=MESH,
        )

    for d in range(1, no):
        copy = t_copy(o, other("ori", d), d)
        copy.start()
        pending.append(copy)
    peaks, masses = [peak], [mass]
    for d in range(1, no):
        od = other("ori", d)
        t_copy(od, od, 0).wait_recv()
        got = stat_r[od]
        peaks.append(got[:, 0:1])
        masses.append(got[:, 64:65])
    top = functools.reduce(jnp.maximum, peaks)
    weight = sum(s * jnp.exp(p - top) for p, s in zip(peaks, masses))
    out[...] = score - (top + jnp.log(weight))
    for copy in pending:
        copy.wait_send()


def body(counts, slice_codes, pixel_mask):
    nm, nf, no = (lax.axis_size(a) for a in ("mod", "frm", "ori"))
    fr, rows, lanes = counts.shape
    orient, band, _ = slice_codes.shape
    group = no * fr
    share = group // nm
    depth = band * lanes
    high = rows + 2 * PASSES
    dims = (nm, nf, no, fr, rows, orient, band)
    dma = pltpu.SemaphoreType.DMA
    f32, bf16 = jnp.float32, jnp.bfloat16
    vmem = pl.BlockSpec(memory_space=pltpu.VMEM)
    result = pl.pallas_call(
        functools.partial(kernel, dims),
        out_shape=jax.ShapeDtypeStruct((share, orient), f32),
        in_specs=[vmem, pl.BlockSpec(memory_space=pl.ANY), vmem],
        out_specs=vmem,
        scratch_shapes=[
            pltpu.VMEM((orient * band, lanes), jnp.int32),
            pltpu.VMEM((orient, depth), bf16),
            pltpu.VMEM((high + STRIDE_ROWS, fr, lanes), f32),
            pltpu.VMEM((2, PASSES, fr, lanes), bf16),
            pltpu.VMEM((2, PASSES, fr, lanes), bf16),
            pltpu.VMEM((nf * fr, depth), bf16),
            pltpu.VMEM((nf * group, depth), bf16),
            pltpu.VMEM((nf * group, orient), f32),
            pltpu.VMEM((nf * group, orient), f32),
            pltpu.VMEM((nm, share, orient), f32),
            pltpu.VMEM((share, 128), f32),
            pltpu.VMEM((no, share, 128), f32),
            pltpu.VMEM((1, orient), f32),
            dma((orient // SLICE_CHUNK,)),
            dma((2,)),
            dma((2,)),
            dma((GROUPS,)),
            dma((GROUPS * nf * (no + 1),)),
            dma((nf * no, GROUPS)),
            dma((nf * nm,)),
            dma((nf, nm)),
            dma((nm,)),
            dma((nm,)),
            dma((no,)),
            dma((no,)),
        ],
        compiler_params=pltpu.CompilerParams(collective_id=0, has_side_effects=True),
    )(counts.reshape(fr * rows, lanes), slice_codes.reshape(orient * band, lanes), pixel_mask)
    return result[None]


def solution(mesh):
    in_specs = (P(("frm", "ori"), "mod", None), P("ori", ("mod", "frm"), None), P("mod", None))
    out_specs = P("frm", "mod", "ori")
    return jax.shard_map(body, mesh=mesh, in_specs=in_specs, out_specs=out_specs, check_vma=False)
```
